512 devices in a mesh: ctx: 16 (over x_hi, y, core), exp: 32 (over x_lo, z).
Axes of the slice: x: 4 (x_hi: 2, x_lo: 2; x = x_hi * 2 + x_lo), y: 4, z: 16, core: 2. Of those that a mesh axis runs over, the one named last changes fastest.
Arguments:
- tokens: bfloat16 [4096, 2048], P('exp', 'ctx'), may hold values from -6 to 6
- expert_ids: int32 [4096, 8], P('exp'), may hold values from 0 to 127, all different within a row; in each aligned block of 128 rows (0 to 127, 128 to 255, ...) at most 9 rows name the same one
- route_gates: float32 [4096, 8], P('exp'), may hold values from 0.2 to 1
- w_gate: bfloat16 [128, 2048, 768], P('exp', 'ctx'), may hold values from -0.125 to 0.125
- w_up: bfloat16 [128, 2048, 768], P('exp', 'ctx'), may hold values from -0.125 to 0.125
- w_down: bfloat16 [128, 768, 2048], P('exp', None, 'ctx'), may hold values from -0.21875 to 0.21875
- grad_out: bfloat16 [4096, 2048], P('exp', 'ctx'), may hold values from -6 to 6
Outputs:
- moe_out: bfloat16 [4096, 2048], P('exp', 'ctx')
- grad_tokens: bfloat16 [4096, 2048], P('exp', 'ctx')
- grad_gate: bfloat16 [128, 2048, 768], P('exp', 'ctx')
- grad_up: bfloat16 [128, 2048, 768], P('exp', 'ctx')
- grad_down: bfloat16 [128, 768, 2048], P('exp', None, 'ctx')
The draws below stay inside these ranges and needn't reach their ends.
Inputs may be any that keep to these rules, and one draw needn't show every extreme that they name: `expert_ids`: each row names 8 different experts. Within each aligned block of 128 rows (the rows of one index of exp) no expert is named by more than 9 rows, and in every draw some block has an expert named by exactly 9 rows.
All inputs are finite; a program needn't handle non-finite values.
Results may differ from the reference program's by a relative error of at most 0.025.
Values may be sent and summed in bfloat16 or wider, within the bound.
A program may use at most 64 MiB of HBM per device.

```python
import math
import jax
import jax.numpy as jnp
import numpy as np
from jax import lax

D = 2048
FF = 768
EXPERTS = 128
TOP = 8
TOK_BLK = 128
CAP = 9
TOKENS = 4096
N_CTX = 16
N_EXP = 32


def block_scale(rng, shape, pieces, low, top_value):
    level, own = 1.0, jax.random.fold_in(rng, 6)
    for dim, parts in pieces:
        steps = jnp.exp(jax.random.uniform(jax.random.fold_in(own, dim), (parts,), jnp.float32, low / len(pieces), top_value / len(pieces)))
        level = level * jnp.repeat(steps, shape[dim] // parts).reshape([-1 if axis == dim else 1 for axis in range(len(shape))])
    return level


def assign_block(own_key, own, number, rows, number_of, top, reach, lean):
    sequence = jax.random.permutation(own_key, number_of)
    crowded, common = shares(number_of, rows * top, reach, lean, True), shares(number_of, rows * top, reach, lean, False)
    places = jnp.arange(number_of)

    def named(tallies, offset_by):
        used = int((tallies > 0).sum())
        fixed = max(1, used // 4)
        moved = fixed + (places - fixed + offset_by * (used - fixed)) % max(1, number_of - fixed)
        return jnp.zeros((number_of,), jnp.int32).at[sequence[jnp.where(places < fixed, places, moved)]].set(jnp.asarray(tallies, jnp.int32))

    tallies = jnp.where(number % 4 == 0, named(crowded, number // 4), named(common, number - number // 4 - 1))
    mixed = jax.random.permutation(jax.random.fold_in(own, 3), number_of)
    donor, receiver = mixed[0:number_of // 2 * 2:2], mixed[1:number_of // 2 * 2:2]
    room = jnp.minimum(tallies[donor] - 1, reach - tallies[receiver]) // 2
    room = jnp.where((donor == sequence[0]) | (receiver == sequence[0]) | (tallies[receiver] == 0), 0, jnp.maximum(room, 0))
    moved = jax.random.randint(jax.random.fold_in(own, 4), (number_of // 2,), 0, 1 << 20) % (room + 1)
    tallies = tallies.at[donor].add(-moved).at[receiver].add(moved)
    labels = jnp.searchsorted(jnp.cumsum(tallies), jnp.arange(rows * top), side="right").astype(jnp.int32)
    listing = labels.reshape(top, rows).T
    listing = listing[jax.random.permutation(jax.random.fold_in(own, 1), rows)]
    offset_by = jax.random.randint(jax.random.fold_in(own, 2), (rows, 1), 0, top)
    return jnp.take_along_axis(listing, (jnp.arange(top)[None, :] + offset_by) % top, axis=1)


def shares(amount, total, most, skew, full):
    loads = [(1 << 20) // math.isqrt(grade ** skew) + 1 for grade in range(1, amount + 1)]
    largest = most if full else min(most, max(-(-total // amount), total * loads[0] // sum(loads)))
    least = 1 if total - largest >= amount - 1 else 0
    holding, rest = [largest] + [least] * (amount - 1), total - largest - least * (amount - 1)
    while rest > 0:
        free = [i for i in range(1, amount) if holding[i] < largest] or [i for i in range(1, amount) if holding[i] < most]
        whole, left = sum([loads[i] for i in free]), rest
        for i in free:
            addition = min(most - holding[i], max(1, left * loads[i] // whole), rest)
            holding[i] = holding[i] + addition
            rest = rest - addition
    return np.array(holding)


def noise(own_key, dims, spread, bound, shards=(), kind=jnp.bfloat16):
    factor_of = block_scale(own_key, dims, shards, -0.22, 0.18) if shards else 1.0
    values = jax.random.normal(own_key, dims, jnp.float32) * spread * factor_of
    return jnp.minimum(jnp.maximum(values, -bound), bound).astype(kind)


def setup_inputs(seed: int = 0) -> dict:
    key_of = jax.random.split(jax.random.key(seed), 8)
    tokens = noise(key_of[0], (TOKENS, D), 1.0, 6.0, ((0, 32), (1, 16)))
    expert_ids_keys = jax.random.split(jax.random.fold_in(key_of[1], 1), TOKENS // TOK_BLK)
    expert_ids_turns = jax.random.permutation(jax.random.fold_in(key_of[1], 3), TOKENS // TOK_BLK)
    expert_ids = jax.vmap(lambda own, number: assign_block(jax.random.fold_in(key_of[1], 2), own, number, TOK_BLK, EXPERTS, TOP, CAP, 2))(expert_ids_keys, expert_ids_turns).reshape((TOKENS, TOP))
    route_gates = jnp.clip(0.2 + 0.8 * jax.random.uniform(key_of[2], (TOKENS, TOP), jnp.float32) ** block_scale(key_of[2], (TOKENS, TOP), ((0, 32),), -0.2, 0.2), 0.2, 1.0)
    w_gate = noise(key_of[3], (EXPERTS, D, FF), D ** -0.5, 0.125, ((0, 32), (1, 16)))
    w_up = noise(key_of[4], (EXPERTS, D, FF), D ** -0.5, 0.125, ((0, 32), (1, 16)))
    w_down = noise(key_of[5], (EXPERTS, FF, D), FF ** -0.5, 0.21875, ((0, 32), (2, 16)))
    grad_out = noise(key_of[6], (TOKENS, D), 1.0, 6.0, ((0, 32), (1, 16)))
    return dict(tokens=tokens, expert_ids=expert_ids, route_gates=route_gates, w_gate=w_gate, w_up=w_up, w_down=w_down, grad_out=grad_out)


def rounded_sum(partial_part):
    held = lax.optimization_barrier(partial_part.astype(jnp.bfloat16))
    return jnp.sum(held.astype(jnp.float32), axis=1)


def reference(tokens, expert_ids, route_gates, w_gate, w_up, w_down, grad_out):
    routes = TOKENS * TOP
    slot_rows = N_EXP * CAP
    local_width = D // N_CTX
    flat_ids = expert_ids.reshape(routes).astype(jnp.int32)
    owner_tok = jnp.arange(routes, dtype=jnp.int32) // TOP
    expert_hit = (flat_ids.reshape(N_EXP, TOK_BLK * TOP)[:, :, None] == jnp.arange(EXPERTS, dtype=jnp.int32)[None, None, :]).astype(jnp.int32)
    earlier = jnp.cumsum(expert_hit, axis=1) - expert_hit
    position = jnp.sum(earlier * expert_hit, axis=2).reshape(routes)
    slot_place = (owner_tok // TOK_BLK) * CAP + position
    flat_slot = (flat_ids * slot_rows + slot_place).astype(jnp.int32)
    slot_table = jnp.full((EXPERTS * slot_rows,), routes, jnp.int32).at[flat_slot].set(jnp.arange(routes, dtype=jnp.int32))
    source_tok = jnp.concatenate([owner_tok, jnp.array([TOKENS], jnp.int32)])[slot_table]
    padded_x = jnp.concatenate([tokens, jnp.zeros((1, D), tokens.dtype)], axis=0)
    rows_x = padded_x[source_tok].reshape(EXPERTS, slot_rows, D)
    scaled = (route_gates[:, :, None].astype(jnp.float32) * grad_out[:, None, :].astype(jnp.float32)).astype(jnp.bfloat16).reshape(routes, D)
    padded_g = jnp.concatenate([scaled, jnp.zeros((1, D), scaled.dtype)], axis=0)
    rows_g = padded_g[slot_table].reshape(EXPERTS, slot_rows, D)

    def one_expert(expert_item):
        exp_x, exp_g, gate_w, up_w, down_w = expert_item
        split_x = exp_x.reshape(slot_rows, N_CTX, local_width).astype(jnp.float32)
        split_g = exp_g.reshape(slot_rows, N_CTX, local_width).astype(jnp.float32)
        gate_split = gate_w.reshape(N_CTX, local_width, FF).astype(jnp.float32)
        up_split = up_w.reshape(N_CTX, local_width, FF).astype(jnp.float32)
        down_split = down_w.reshape(FF, N_CTX, local_width).astype(jnp.float32)
        gate_sum = rounded_sum(jnp.einsum("mcd,cdf->mcf", split_x, gate_split))
        up_sum = rounded_sum(jnp.einsum("mcd,cdf->mcf", split_x, up_split))
        back_sum = rounded_sum(jnp.einsum("mcd,fcd->mcf", split_g, down_split))
        sigmoid_gate = jax.nn.sigmoid(gate_sum)
        silu_gate = gate_sum * sigmoid_gate
        hidden = (silu_gate * up_sum).astype(jnp.bfloat16)
        grad_gate_rows = (back_sum * up_sum * sigmoid_gate * (1.0 + gate_sum * (1.0 - sigmoid_gate))).astype(jnp.bfloat16)
        grad_up_rows = (back_sum * silu_gate).astype(jnp.bfloat16)
        expert_out = jnp.dot(hidden, down_w, preferred_element_type=jnp.float32).astype(jnp.bfloat16)
        expert_back = (jnp.dot(grad_gate_rows, gate_w.T, preferred_element_type=jnp.float32) + jnp.dot(grad_up_rows, up_w.T, preferred_element_type=jnp.float32)).astype(jnp.bfloat16)
        grad_gate_w = jnp.dot(exp_x.T, grad_gate_rows, preferred_element_type=jnp.float32).astype(jnp.bfloat16)
        grad_up_w = jnp.dot(exp_x.T, grad_up_rows, preferred_element_type=jnp.float32).astype(jnp.bfloat16)
        grad_down_w = jnp.dot(hidden.T, exp_g, preferred_element_type=jnp.float32).astype(jnp.bfloat16)
        return expert_out, expert_back, grad_gate_w, grad_up_w, grad_down_w

    results = lax.map(one_expert, (rows_x, rows_g, w_gate, w_up, w_down))
    expert_out, expert_back, grad_gate, grad_up, grad_down = results
    picked_out = expert_out.reshape(EXPERTS * slot_rows, D)[flat_slot].astype(jnp.float32).reshape(TOKENS, TOP, D)
    picked_back = expert_back.reshape(EXPERTS * slot_rows, D)[flat_slot].astype(jnp.float32).reshape(TOKENS, TOP, D)
    moe_out = jnp.sum(route_gates[:, :, None].astype(jnp.float32) * picked_out, axis=1).astype(jnp.bfloat16)
    grad_tokens = jnp.sum(picked_back, axis=1).astype(jnp.bfloat16)
    return (moe_out, grad_tokens, grad_gate, grad_up, grad_down)
```

```python
import jax
import jax.numpy as jnp
from jax import lax
from jax.experimental import pallas as pl
from jax.experimental.pallas import tpu as pltpu
from jax.sharding import PartitionSpec as P

CAP = 9
MESH = pl.DeviceIdType.MESH
BF = jnp.bfloat16
F32 = jnp.float32

TOK = 128
LN = 128
FF = 768
NEXP = 32
NK = 8
GRP = 4
COLS = 5
PR = 16
SLOTS = 18
CH = 3
CW = FF // CH
SH = 144
ORDER = [(x, z) for z in (8, 7, 9, 6, 10, 5, 11, 4, 12, 3, 13, 2, 14, 1, 15) for x in (1, 0)] + [(1, 0)]


def dot(a, b):
    return lax.dot_general(a, b, (((1,), (0,)), ((), ())), preferred_element_type=F32)


def dot_tn(a, b):
    return lax.dot_general(a, b, (((0,), (0,)), ((), ())), preferred_element_type=F32)


def dot_nt(a, b):
    return lax.dot_general(a, b, (((1,), (1,)), ((), ())), preferred_element_type=F32)


def iota(shape, dim):
    return lax.broadcasted_iota(jnp.int32, shape, dim)


def packet_target(q, index):
    col = (index >= 128).astype(jnp.int32)
    rest = index - 128 * col
    source = rest // PR
    place = PR * (q + col) + rest % PR - SLOTS * q
    second = (place >= CAP).astype(jnp.int32)
    target = second * 72 + source * CAP + place - CAP * second
    return jnp.where((place >= 0) & (place < SLOTS), target, -1)


def kernel(
    tok_ref, ids_ref, gates_ref, wg_ref, wu_ref, wd_ref, gout_ref,
    out_ref, gtok_ref, gg_ref, gu_ref, gd_ref,
    xg, wgb, wub, wdb, pos_t, gate_t, pick, slot_gate, perm, perm_t,
    send_d, recv_d, rows_x, rows_g, part, recv_p, hid, acc_o, acc_b,
    send_r, recv_r, grad_g, grad_u, grad_d, fin, recv_f,
    sem_loc, sem_cs, sem_cr, sem_ds, sem_dr, sem_ps, sem_pr, sem_hs, sem_hr,
    sem_rs, sem_rr, sem_fs, sem_fr,
):
    ctx = lax.axis_index("ctx")
    exp = lax.axis_index("exp")
    core = ctx % 2
    other = 1 - core
    chip = ctx // 2
    x_lo = exp // 16
    z_at = exp % 16
    partner = 2 * chip + other

    def exp_at(x, z):
        return ((x_lo + x) % 2) * 16 + (z_at + z) % 16

    def chip_at(d):
        return (chip + d) % NK

    barrier = pltpu.get_barrier_semaphore()
    pl.semaphore_signal(barrier, 1, device_id=(partner, exp), device_id_type=MESH)
    for x, z in ORDER:
        pl.semaphore_signal(barrier, 1, device_id=(ctx, exp_at(x, z)), device_id_type=MESH)
    for d in range(1, NK):
        pl.semaphore_signal(
            barrier, 1, device_id=(2 * chip_at(d) + core, exp), device_id_type=MESH
        )

    local = [
        pltpu.make_async_copy(tok_ref, xg.at[core], sem_loc.at[0]),
        pltpu.make_async_copy(gout_ref, xg.at[2 + core], sem_loc.at[1]),
        pltpu.make_async_copy(wg_ref.at[pl.ds(2 * core, 2)], wgb.at[core], sem_loc.at[2]),
        pltpu.make_async_copy(wu_ref.at[pl.ds(2 * core, 2)], wub.at[core], sem_loc.at[3]),
        pltpu.make_async_copy(wd_ref.at[pl.ds(2 * core, 2)], wdb.at[core], sem_loc.at[4]),
    ]
    for cp in local:
        cp.start()

    lane = iota((TOK, 128), 1)
    expert = jnp.where(lane < 64, 4 * (lane % 32) + 2 * core + lane // 32, -1)
    hit = jnp.zeros((TOK, 128), F32)
    gate = jnp.zeros((TOK, 128), F32)
    for k in range(8):
        same = ids_ref[:, k : k + 1] == expert
        hit = hit + same.astype(F32)
        gate = gate + jnp.where(same, gates_ref[:, k : k + 1], 0.0)
    earlier = (iota((TOK, TOK), 1) < iota((TOK, TOK), 0)).astype(F32).astype(BF)
    place = dot(earlier, hit.astype(BF))
    pos_t[...] = jnp.where(hit > 0.5, place, -1.0).T
    gate_t[...] = gate.T

    def build(d, carry):
        p0 = pos_t[pl.ds(d, 1), :]
        p1 = pos_t[pl.ds(d + NEXP, 1), :]
        g0 = gate_t[pl.ds(d, 1), :]
        g1 = gate_t[pl.ds(d + NEXP, 1), :]
        at = pl.ds(pl.multiple_of(d * PR, PR), PR)
        for c in range(COLS):
            row = iota((PR, TOK), 0) + PR * c
            quarter = jnp.where(row >= SLOTS * c, c, c - 1)
            slot = row - SLOTS * quarter
            second = slot >= CAP
            wanted = jnp.where(second, slot - CAP, slot).astype(F32)
            if c == COLS - 1:
                wanted = jnp.where(row < 4 * SLOTS, wanted, -2.0)
            chosen = jnp.where(second, p1, p0) == wanted
            pick[c, at, :] = chosen.astype(F32).astype(BF)
            weight = jnp.sum(
                jnp.where(chosen, jnp.where(second, g1, g0), 0.0), axis=1, keepdims=True
            )
            slot_gate[c, at, :] = jnp.broadcast_to(weight, (PR, 128))
        return carry

    lax.fori_loop(0, NEXP, build, 0)
    for q in range(4):
        perm[q] = (packet_target(q, iota((SH, 256), 1)) == iota((SH, 256), 0)).astype(F32).astype(BF)
        perm_t[q] = (
            (packet_target(q, iota((256, SH), 0)) == iota((256, SH), 1)).astype(F32).astype(BF)
        )

    for cp in local:
        cp.wait()
    pl.semaphore_wait(barrier, 1 + len(ORDER) + NK - 1)

    def to_partner(i, src, dst):
        return pltpu.make_async_remote_copy(
            src, dst, sem_cs.at[i], sem_cr.at[i], device_id=(partner, exp), device_id_type=MESH
        )

    tok_cp = [to_partner(0, tok_ref, xg.at[core]), to_partner(1, gout_ref, xg.at[2 + core])]
    w_cp = [
        to_partner(2, wg_ref.at[pl.ds(2 * other, 2)], wgb.at[core]),
        to_partner(3, wu_ref.at[pl.ds(2 * other, 2)], wub.at[core]),
        to_partner(4, wd_ref.at[pl.ds(2 * other, 2)], wdb.at[core]),
    ]
    for cp in tok_cp + w_cp:
        cp.start()
    for cp in tok_cp:
        cp.wait_recv()

    packet_row = iota((NEXP * PR, LN), 0) % PR
    for c in range(COLS):
        low = packet_row < 2 * c
        if c == 0:
            rows = dot(pick[c], xg[0])
        elif c == COLS - 1:
            rows = dot(pick[c], xg[3])
        else:
            both = dot(pick[c], jnp.concatenate([xg[c - 1], xg[c]], axis=1))
            rows = jnp.where(low, both[:, :LN], both[:, LN:])
        if c == 2:
            rows = rows * jnp.where(low, 1.0, slot_gate[c])
        elif c > 2:
            rows = rows * slot_gate[c]
        send_d[:, :, c * LN : (c + 1) * LN] = rows.astype(BF).reshape(NEXP, PR, LN)

    def exp_copies(src, dst, sem_s, sem_r):
        return [
            pltpu.make_async_remote_copy(
                src.at[exp_at(x, z)], dst.at[exp], sem_s.at[i], sem_r.at[exp],
                device_id=(ctx, exp_at(x, z)), device_id_type=MESH,
            )
            for i, (x, z) in enumerate(ORDER)
        ]

    d_own = pltpu.make_async_copy(send_d.at[exp], recv_d.at[exp], sem_dr.at[exp])
    d_cp = exp_copies(send_d, recv_d, sem_ds, sem_dr)
    for cp in d_cp:
        cp.start()
    d_own.start()
    for cp in w_cp:
        cp.wait_recv()
    for j in range(NEXP):
        pltpu.make_async_copy(send_d.at[j], recv_d.at[j], sem_dr.at[j]).wait()

    for q in range(4):
        for pair in range(2):
            cols = []
            for g in (2 * pair, 2 * pair + 1):
                cols.append(
                    jnp.concatenate(
                        [
                            recv_d[8 * g : 8 * g + 8, :, c * LN : (c + 1) * LN].reshape(128, LN)
                            for c in (q, q + 1)
                        ],
                        axis=0,
                    )
                )
            got = dot(perm[q], jnp.concatenate(cols, axis=1))
            into = rows_x if q < 2 else rows_g
            for e in range(2):
                into[e, pair * SH : (pair + 1) * SH, (q % 2) * LN : (q % 2 + 1) * LN] = (
                    jnp.concatenate(
                        [got[e * 72 : e * 72 + 72, :LN], got[e * 72 : e * 72 + 72, LN:]], axis=0
                    ).astype(BF)
                )

    def w_cols(ref, e, ch):
        at = slice(ch * CW, (ch + 1) * CW)
        return jnp.concatenate([ref[0, e, :, at], ref[1, e, :, at]], axis=0)

    def w_rows(e, ch):
        at = slice(ch * CW, (ch + 1) * CW)
        return jnp.concatenate([wdb[0, e, at, :], wdb[1, e, at, :]], axis=1)

    def chip_copies(ch, src_of, dst_of, sem_s, sem_r):
        return [
            pltpu.make_async_remote_copy(
                src_of(d), dst_of(d), sem_s.at[ch, d - 1], sem_r.at[ch, d - 1],
                device_id=(2 * chip_at(d) + core, exp), device_id_type=MESH,
            )
            for d in range(1, NK)
        ]

    p_cp = []
    for ch in range(CH):
        for e in range(2):
            made = (
                dot(rows_x[e], w_cols(wgb, e, ch)),
                dot(rows_x[e], w_cols(wub, e, ch)),
                dot_nt(rows_g[e], w_rows(e, ch)),
            )
            for n, value in enumerate(made):
                value = value.astype(BF)
                for half in range(2):
                    for side in range(2):
                        part[ch, (2 * e + half) * 2 + side, :, n * LN : (n + 1) * LN] = value[
                            half * SH : (half + 1) * SH, side * LN : (side + 1) * LN
                        ]
        cps = chip_copies(
            ch, lambda d: part.at[ch, chip_at(d)], lambda d: recv_p.at[ch, d - 1], sem_ps, sem_pr
        )
        for cp in cps:
            cp.start()
        p_cp.append(cps)

    h_cp = []
    for ch in range(CH):
        for cp in p_cp[ch]:
            cp.wait_recv()
        sums = []
        for n in range(3):
            at = slice(n * LN, (n + 1) * LN)
            total = part[ch, chip, :, at].astype(F32)
            for d in range(NK - 1):
                total = total + recv_p[ch, d, :, at].astype(F32)
            sums.append(total)
        gate_sum, up_sum, back_sum = sums
        sig = jax.nn.sigmoid(gate_sum)
        silu = gate_sum * sig
        hid[ch, chip, :, 0:LN] = (silu * up_sum).astype(BF)
        hid[ch, chip, :, LN : 2 * LN] = (
            back_sum * up_sum * sig * (1.0 + gate_sum * (1.0 - sig))
        ).astype(BF)
        hid[ch, chip, :, 2 * LN : 3 * LN] = (back_sum * silu).astype(BF)
        cps = chip_copies(
            ch, lambda d: hid.at[ch, chip], lambda d: hid.at[ch, chip], sem_hs, sem_hr
        )
        for cp in cps:
            cp.start()
        h_cp.append(cps)

    def hid_rows(ch, e, n):
        at = slice(n * LN, (n + 1) * LN)
        return jnp.concatenate(
            [
                jnp.concatenate([hid[ch, (2 * e + half) * 2 + side, :, at] for side in range(2)], axis=1)
                for half in range(2)
            ],
            axis=0,
        )

    for ch in range(CH):
        for cp in h_cp[ch]:
            cp.wait_recv()
        at = slice(ch * CW, (ch + 1) * CW)
        for e in range(2):
            h, g, u = (hid_rows(ch, e, n) for n in range(3))
            o = dot(h, w_rows(e, ch))
            b = dot_nt(g, w_cols(wgb, e, ch)) + dot_nt(u, w_cols(wub, e, ch))
            if ch == 0:
                acc_o[e] = o
                acc_b[e] = b
            else:
                acc_o[e] += o
                acc_b[e] += b
            dg = dot_tn(rows_x[e], g).astype(BF)
            du = dot_tn(rows_x[e], u).astype(BF)
            dd = dot_tn(h, rows_g[e]).astype(BF)
            for half in range(2):
                grad_g[half, e, :, at] = dg[half * LN : (half + 1) * LN]
                grad_u[half, e, :, at] = du[half * LN : (half + 1) * LN]
                grad_d[half, e, at, :] = dd[:, half * LN : (half + 1) * LN]

    def back_rows(q):
        ref = acc_o if q < 2 else acc_b
        at = slice((q % 2) * LN, (q % 2 + 1) * LN)
        return jnp.concatenate(
            [
                jnp.concatenate(
                    [ref[e, g * 72 : g * 72 + 72, at] for e in range(2)], axis=0
                ).astype(BF)
                for g in range(GRP)
            ],
            axis=1,
        )

    back = [back_rows(q) for q in range(4)]
    for c in range(COLS):
        value = None
        for q in (c - 1, c):
            if 0 <= q < 4:
                term = dot(perm_t[q, (c - q) * 128 : (c - q + 1) * 128, :], back[q])
                value = term if value is None else value + term
        value = value.astype(BF)
        for g in range(GRP):
            send_r[8 * g : 8 * g + 8, :, c * LN : (c + 1) * LN] = value[
                :, g * LN : (g + 1) * LN
            ].reshape(8, PR, LN)
    r_own = pltpu.make_async_copy(send_r.at[exp], recv_r.at[exp], sem_rr.at[exp])
    r_cp = exp_copies(send_r, recv_r, sem_rs, sem_rr)
    for cp in r_cp:
        cp.start()
    r_own.start()

    mine = pl.ds(2 * core, 2)
    g_own = [
        pltpu.make_async_copy(grad_g.at[core], gg_ref.at[mine], sem_loc.at[0]),
        pltpu.make_async_copy(grad_u.at[core], gu_ref.at[mine], sem_loc.at[1]),
        pltpu.make_async_copy(grad_d.at[core], gd_ref.at[mine], sem_loc.at[2]),
    ]
    g_cp = [
        to_partner(5, grad_g.at[other], gg_ref.at[mine]),
        to_partner(6, grad_u.at[other], gu_ref.at[mine]),
        to_partner(7, grad_d.at[other], gd_ref.at[mine]),
    ]
    for cp in g_own + g_cp:
        cp.start()
    for j in range(NEXP):
        pltpu.make_async_copy(send_r.at[j], recv_r.at[j], sem_rr.at[j]).wait()

    sums = [None] * 4
    for c in range(COLS):
        value = recv_r[:, :, c * LN : (c + 1) * LN].reshape(NEXP * PR, LN).astype(F32)
        low = packet_row < 2 * c
        if c < 2:
            value = value * slot_gate[c]
        elif c == 2:
            value = value * jnp.where(low, slot_gate[c], 1.0)
        first = jnp.where(low, value, 0.0).astype(BF)
        second = jnp.where(low, 0.0, value).astype(BF)
        if c == 0:
            sums[0] = dot_tn(pick[c], second)
        elif c == COLS - 1:
            sums[3] = sums[3] + dot_tn(pick[c], first)
        else:
            got = dot_tn(pick[c], jnp.concatenate([first, second], axis=1))
            sums[c - 1] = sums[c - 1] + got[:, :LN]
            sums[c] = got[:, LN:]
    for q in range(4):
        fin[q] = sums[q]
    f_cp = [
        pltpu.make_async_remote_copy(
            fin.at[2 * i + other], recv_f.at[i], sem_fs.at[i], sem_fr.at[i],
            device_id=(partner, exp), device_id_type=MESH,
        )
        for i in range(2)
    ]
    for cp in f_cp:
        cp.start()
    for cp in tok_cp + w_cp:
        cp.wait_send()
    for cp in d_cp + r_cp:
        cp.wait_send()
    for cps in p_cp + h_cp:
        for cp in cps:
            cp.wait_send()
    for cp in g_own:
        cp.wait()
    for cp in g_cp:
        cp.wait()
    for cp in f_cp:
        cp.wait()
    out_ref[...] = (fin[core] + recv_f[0]).astype(BF)
    gtok_ref[...] = (fin[2 + core] + recv_f[1]).astype(BF)


def per_device(tokens, expert_ids, route_gates, w_gate, w_up, w_down, grad_out):
    vmem = pl.BlockSpec(memory_space=pltpu.VMEM)
    dma = pltpu.SemaphoreType.DMA
    return pl.pallas_call(
        kernel,
        out_shape=(
            jax.ShapeDtypeStruct((TOK, LN), BF),
            jax.ShapeDtypeStruct((TOK, LN), BF),
            jax.ShapeDtypeStruct((4, LN, FF), BF),
            jax.ShapeDtypeStruct((4, LN, FF), BF),
            jax.ShapeDtypeStruct((4, FF, LN), BF),
        ),
        in_specs=[vmem] * 7,
        out_specs=(vmem,) * 5,
        scratch_shapes=[
            pltpu.VMEM((4, TOK, LN), BF),
            pltpu.VMEM((2, 2, LN, FF), BF),
            pltpu.VMEM((2, 2, LN, FF), BF),
            pltpu.VMEM((2, 2, FF, LN), BF),
            pltpu.VMEM((128, TOK), F32),
            pltpu.VMEM((128, TOK), F32),
            pltpu.VMEM((COLS, NEXP * PR, TOK), BF),
            pltpu.VMEM((COLS, NEXP * PR, LN), F32),
            pltpu.VMEM((4, SH, 256), BF),
            pltpu.VMEM((4, 256, SH), BF),
            pltpu.VMEM((NEXP, PR, COLS * LN), BF),
            pltpu.VMEM((NEXP, PR, COLS * LN), BF),
            pltpu.VMEM((2, 2 * SH, 2 * LN), BF),
            pltpu.VMEM((2, 2 * SH, 2 * LN), BF),
            pltpu.VMEM((CH, NK, SH, 3 * LN), BF),
            pltpu.VMEM((CH, NK - 1, SH, 3 * LN), BF),
            pltpu.VMEM((CH, NK, SH, 3 * LN), BF),
            pltpu.VMEM((2, 2 * SH, 2 * LN), F32),
            pltpu.VMEM((2, 2 * SH, 2 * LN), F32),
            pltpu.VMEM((NEXP, PR, COLS * LN), BF),
            pltpu.VMEM((NEXP, PR, COLS * LN), BF),
            pltpu.VMEM((2, 2, LN, FF), BF),
            pltpu.VMEM((2, 2, LN, FF), BF),
            pltpu.VMEM((2, 2, FF, LN), BF),
            pltpu.VMEM((4, TOK, LN), F32),
            pltpu.VMEM((2, TOK, LN), F32),
            dma((5,)),
            dma((8,)),
            dma((8,)),
            dma((len(ORDER),)),
            dma((NEXP,)),
            dma((CH, NK - 1)),
            dma((CH, NK - 1)),
            dma((CH, NK - 1)),
            dma((CH, NK - 1)),
            dma((len(ORDER),)),
            dma((NEXP,)),
            dma((2,)),
            dma((2,)),
        ],
        compiler_params=pltpu.CompilerParams(collective_id=0, has_side_effects=True),
        name="moe_block",
    )(tokens, expert_ids, route_gates, w_gate, w_up, w_down, grad_out)


def solution(mesh):
    return jax.shard_map(
        per_device,
        mesh=mesh,
        in_specs=(
            P("exp", "ctx"),
            P("exp", None),
            P("exp", None),
            P("exp", "ctx", None),
            P("exp", "ctx", None),
            P("exp", None, "ctx"),
            P("exp", "ctx"),
        ),
        out_specs=(
            P("exp", "ctx"),
            P("exp", "ctx"),
            P("exp", "ctx", None),
            P("exp", "ctx", None),
            P("exp", None, "ctx"),
        ),
        check_vma=False,
    )
```

```python
import jax
import jax.numpy as jnp
from jax import lax
from jax.experimental import pallas as pl
from jax.experimental.pallas import tpu as pltpu
from jax.sharding import PartitionSpec as P

CAP = 9
MESH = pl.DeviceIdType.MESH
BF = jnp.bfloat16
F32 = jnp.float32

TOK = 128
LN = 128
FF = 768
NEXP = 32
GRP = 4
COLS = 5
PR = 16
SLOTS = 18
SH = 72
HALF = FF // 2
OFFS = [
    (0, 0), (1, 0), (0, 1), (1, 1), (0, 15), (1, 15), (0, 2), (1, 2),
    (0, 8), (1, 8), (0, 7), (1, 7), (0, 9), (1, 9), (0, 6), (1, 6),
    (0, 10), (1, 10), (0, 5), (1, 5), (0, 11), (1, 11), (0, 12), (1, 12),
    (0, 4), (1, 4), (0, 3), (1, 3), (0, 13), (1, 13), (0, 14), (1, 14),
]
STEPS = "D0 D1 S0 F0 S1 D2 F1 O0 D3 S2 F2 O1 S3 F3 O2 O3".split()


def dot(a, b):
    return lax.dot_general(a, b, (((1,), (0,)), ((), ())), preferred_element_type=F32)


def dot_tn(a, b):
    return lax.dot_general(a, b, (((0,), (0,)), ((), ())), preferred_element_type=F32)


def dot_nt(a, b):
    return lax.dot_general(a, b, (((1,), (1,)), ((), ())), preferred_element_type=F32)


def iota(shape, dim):
    return lax.broadcasted_iota(jnp.int32, shape, dim)


def packet_target(q, index):
    col = (index >= 128).astype(jnp.int32)
    rest = index - 128 * col
    source = rest // PR
    place = PR * (q + col) + rest % PR - SLOTS * q
    second = (place >= CAP).astype(jnp.int32)
    target = second * 72 + source * CAP + place - CAP * second
    return jnp.where((place >= 0) & (place < SLOTS), target, -1)


def kernel(
    tok_ref, ids_ref, gates_ref, wg_ref, wu_ref, wd_ref, gout_ref,
    out_ref, gtok_ref, gg_ref, gu_ref, gd_ref,
    xg, wgb, wub, wdb, pos_t, gate_t, pick, slot_gate, perm, perm_t,
    send_d, recv_d, rows_x, rows_g, part, recv_p, sum_s, sum_r, hid,
    send_r, recv_r, grad_g, grad_u, grad_d, fin, recv_f,
    sem_loc, sem_cs, sem_cr, sem_ds, sem_dr, sem_ps, sem_pr, sem_xs, sem_xr, sem_hs, sem_hr,
    sem_rs, sem_rr, sem_fs, sem_fr,
):
    ctx = lax.axis_index("ctx")
    exp = lax.axis_index("exp")
    core = ctx % 2
    other = 1 - core
    y_at = (ctx // 2) % 4
    x_hi = ctx // 8
    x_lo = exp // 16
    z_at = exp % 16
    partner = ctx - core + other
    across = ctx - 8 * x_hi + 8 * (1 - x_hi)

    def exp_at(x, z):
        return ((x_lo + x) % 2) * 16 + (z_at + z) % 16

    def y_dev(d):
        return 8 * x_hi + 2 * ((y_at + d) % 4) + core

    barrier = pltpu.get_barrier_semaphore()
    pl.semaphore_signal(barrier, 1, device_id=(partner, exp), device_id_type=MESH)
    for x, z in OFFS[::-1]:
        if (x, z) != (0, 0):
            pl.semaphore_signal(barrier, 1, device_id=(ctx, exp_at(x, z)), device_id_type=MESH)
    for d in range(1, 4):
        pl.semaphore_signal(barrier, 1, device_id=(y_dev(d), exp), device_id_type=MESH)
    pl.semaphore_signal(barrier, 1, device_id=(across, exp), device_id_type=MESH)

    local = [
        pltpu.make_async_copy(tok_ref, xg.at[core], sem_loc.at[0]),
        pltpu.make_async_copy(gout_ref, xg.at[2 + core], sem_loc.at[1]),
        pltpu.make_async_copy(wg_ref.at[pl.ds(2 * core, 2)], wgb.at[core], sem_loc.at[2]),
        pltpu.make_async_copy(wu_ref.at[pl.ds(2 * core, 2)], wub.at[core], sem_loc.at[3]),
        pltpu.make_async_copy(wd_ref.at[pl.ds(2 * core, 2)], wdb.at[core], sem_loc.at[4]),
    ]
    for cp in local:
        cp.start()

    row = iota((128, TOK), 0)
    expert = jnp.where(row < 64, 4 * (row % 32) + 2 * core + row // 32, -1)
    hit = jnp.zeros((128, TOK), F32)
    gate = jnp.zeros((128, TOK), F32)
    for k in range(8):
        same = ids_ref[k : k + 1, :] == expert
        hit = hit + same.astype(F32)
        gate = gate + jnp.where(same, gates_ref[k : k + 1, :], 0.0)
    earlier = (iota((TOK, TOK), 0) < iota((TOK, TOK), 1)).astype(F32).astype(BF)
    pos_t[...] = jnp.where(hit > 0.5, dot(hit.astype(BF), earlier), -1.0)
    gate_t[...] = gate

    def build(d, carry):
        p0 = pos_t[pl.ds(d, 1), :]
        p1 = pos_t[pl.ds(d + NEXP, 1), :]
        g0 = gate_t[pl.ds(d, 1), :]
        g1 = gate_t[pl.ds(d + NEXP, 1), :]
        at = pl.ds(pl.multiple_of(d * PR, PR), PR)
        for c in range(COLS):
            row = iota((PR, TOK), 0) + PR * c
            quarter = jnp.where(row >= SLOTS * c, c, c - 1)
            slot = row - SLOTS * quarter
            second = slot >= CAP
            wanted = jnp.where(second, slot - CAP, slot).astype(F32)
            if c == COLS - 1:
                wanted = jnp.where(row < 4 * SLOTS, wanted, -2.0)
            chosen = jnp.where(second, p1, p0) == wanted
            pick[c, at, :] = chosen.astype(F32).astype(BF)
            weight = jnp.sum(
                jnp.where(chosen, jnp.where(second, g1, g0), 0.0), axis=1, keepdims=True
            )
            slot_gate[c, at, :] = jnp.broadcast_to(weight, (PR, 128))
        return carry

    lax.fori_loop(0, NEXP, build, 0)
    for q in range(4):
        perm[q] = (
            (packet_target(q, iota((2 * SH, 256), 1)) == iota((2 * SH, 256), 0))
            .astype(F32).astype(BF)
        )
        perm_t[q] = (
            (packet_target(q, iota((256, 2 * SH), 0)) == iota((256, 2 * SH), 1))
            .astype(F32).astype(BF)
        )

    for cp in local:
        cp.wait()
    pl.semaphore_wait(barrier, 1 + (NEXP - 1) + 3 + 1)

    def to_partner(i, src, dst):
        return pltpu.make_async_remote_copy(
            src, dst, sem_cs.at[i], sem_cr.at[i], device_id=(partner, exp), device_id_type=MESH
        )

    tok_cp = [to_partner(0, tok_ref, xg.at[core]), to_partner(1, gout_ref, xg.at[2 + core])]
    w_cp = [
        to_partner(2, wg_ref.at[pl.ds(2 * other, 2)], wgb.at[core]),
        to_partner(3, wu_ref.at[pl.ds(2 * other, 2)], wub.at[core]),
        to_partner(4, wd_ref.at[pl.ds(2 * other, 2)], wdb.at[core]),
    ]
    for cp in tok_cp + w_cp:
        cp.start()
    for cp in tok_cp:
        cp.wait_recv()

    packet_row = iota((NEXP * PR, LN), 0) % PR
    for c in range(COLS):
        low = packet_row < 2 * c
        if c == 0:
            rows = dot(pick[c], xg[0])
        elif c == COLS - 1:
            rows = dot(pick[c], xg[3])
        else:
            both = dot(pick[c], jnp.concatenate([xg[c - 1], xg[c]], axis=1))
            rows = jnp.where(low, both[:, :LN], both[:, LN:])
        if c == 2:
            rows = rows * jnp.where(low, 1.0, slot_gate[c])
        elif c > 2:
            rows = rows * slot_gate[c]
        send_d[:, :, c * LN : (c + 1) * LN] = rows.astype(BF).reshape(NEXP, PR, LN)

    d_cp = []
    for i, (x, z) in enumerate(OFFS):
        to = exp_at(x, 16 - z)
        if (x, z) == (0, 0):
            cp = pltpu.make_async_copy(send_d.at[exp], recv_d.at[i], sem_dr.at[i])
        else:
            cp = pltpu.make_async_remote_copy(
                send_d.at[to], recv_d.at[i], sem_ds.at[i], sem_dr.at[i],
                device_id=(ctx, to), device_id_type=MESH,
            )
            d_cp.append(cp)
        cp.start()
    for cp in w_cp:
        cp.wait_recv()

    def w_cols(ref, e):
        return jnp.concatenate([ref[0, e], ref[1, e]], axis=0)

    def w_rows(e):
        return jnp.concatenate([wdb[0, e], wdb[1, e]], axis=1)

    def y_copies(s, src_of, dst_of, sem_s, sem_r):
        cps = [
            pltpu.make_async_remote_copy(
                src_of(d), dst_of(d), sem_s.at[s, d - 1], sem_r.at[s, d - 1],
                device_id=(y_dev(d), exp), device_id_type=MESH,
            )
            for d in (2, 1, 3)
        ]
        for cp in cps:
            cp.start()
        return cps

    p_cp, x_cp, h_cp, r_cp = {}, {}, {}, []

    def step_d(s):
        for i in range(8 * s, 8 * s + 8):
            pltpu.make_async_copy(send_d.at[i], recv_d.at[i], sem_dr.at[i]).wait()
        cols = [
            recv_d[8 * s : 8 * s + 8, :, c * LN : (c + 1) * LN].reshape(128, LN)
            for c in range(COLS)
        ]
        for q in range(4):
            got = dot(perm[q], jnp.concatenate(cols[q : q + 2], axis=0))
            into = rows_x if q < 2 else rows_g
            for e in range(2):
                into[s, e, :, (q % 2) * LN : (q % 2 + 1) * LN] = got[
                    e * SH : (e + 1) * SH
                ].astype(BF)
        for e in range(2):
            made = (
                dot(rows_x[s, e], w_cols(wgb, e)),
                dot(rows_x[s, e], w_cols(wub, e)),
                dot_nt(rows_g[s, e], w_rows(e)),
            )
            for n, value in enumerate(made):
                value = value.astype(BF)
                for side in range(2):
                    part[s, 2 * e + side, :, n * HALF : (n + 1) * HALF] = value[
                        :, side * HALF : (side + 1) * HALF
                    ]
        p_cp[s] = y_copies(
            s, lambda d: part.at[s, (y_at + d) % 4], lambda d: recv_p.at[s, d - 1], sem_ps, sem_pr
        )

    def step_s(s):
        for cp in p_cp[s]:
            cp.wait_recv()
        total = part[s, y_at].astype(F32)
        for d in range(3):
            total = total + recv_p[s, d].astype(F32)
        sum_s[s] = total.astype(BF)
        x_cp[s] = pltpu.make_async_remote_copy(
            sum_s.at[s], sum_r.at[s], sem_xs.at[s], sem_xr.at[s],
            device_id=(across, exp), device_id_type=MESH,
        )
        x_cp[s].start()

    def step_f(s):
        x_cp[s].wait_recv()
        total = sum_s[s].astype(F32) + sum_r[s].astype(F32)
        gate_sum, up_sum, back_sum = (total[:, n * HALF : (n + 1) * HALF] for n in range(3))
        sig = jax.nn.sigmoid(gate_sum)
        silu = gate_sum * sig
        hid[s, y_at, :, 0:HALF] = (silu * up_sum).astype(BF)
        hid[s, y_at, :, HALF : 2 * HALF] = (
            back_sum * up_sum * sig * (1.0 + gate_sum * (1.0 - sig))
        ).astype(BF)
        hid[s, y_at, :, 2 * HALF : 3 * HALF] = (back_sum * silu).astype(BF)
        h_cp[s] = y_copies(s, lambda d: hid.at[s, y_at], lambda d: hid.at[s, y_at], sem_hs, sem_hr)

    def hid_rows(s, e, n):
        at = slice(n * HALF, (n + 1) * HALF)
        return jnp.concatenate([hid[s, 2 * e, :, at], hid[s, 2 * e + 1, :, at]], axis=1)

    def step_o(s):
        for cp in h_cp[s]:
            cp.wait_recv()
        made = []
        for e in range(2):
            h, g, u = (hid_rows(s, e, n) for n in range(3))
            made.append(
                (
                    dot(h, w_rows(e)).astype(BF),
                    (dot_nt(g, w_cols(wgb, e)) + dot_nt(u, w_cols(wub, e))).astype(BF),
                )
            )
        back = [
            jnp.concatenate(
                [made[e][q // 2][:, (q % 2) * LN : (q % 2 + 1) * LN].astype(F32) for e in range(2)],
                axis=0,
            ).astype(BF)
            for q in range(4)
        ]
        for c in range(COLS):
            value = None
            for q in (c - 1, c):
                if 0 <= q < 4:
                    term = dot(perm_t[q, (c - q) * 128 : (c - q + 1) * 128, :], back[q])
                    value = term if value is None else value + term
            send_r[8 * s : 8 * s + 8, :, c * LN : (c + 1) * LN] = value.astype(BF).reshape(
                8, PR, LN
            )
        for i in range(8 * s, 8 * s + 8):
            x, z = OFFS[i]
            to = exp_at(x, z)
            if (x, z) == (0, 0):
                cp = pltpu.make_async_copy(send_r.at[i], recv_r.at[exp], sem_rr.at[i])
            else:
                cp = pltpu.make_async_remote_copy(
                    send_r.at[i], recv_r.at[exp], sem_rs.at[i], sem_rr.at[i],
                    device_id=(ctx, to), device_id_type=MESH,
                )
                r_cp.append(cp)
            cp.start()

    do = {"D": step_d, "S": step_s, "F": step_f, "O": step_o}
    for step in STEPS:
        do[step[0]](int(step[1]))

    for e in range(2):
        h, g, u = (
            jnp.concatenate([hid_rows(s, e, n).astype(F32) for s in range(GRP)], axis=0).astype(BF)
            for n in range(3)
        )
        xr, gr = (
            jnp.concatenate([ref[s, e].astype(F32) for s in range(GRP)], axis=0).astype(BF)
            for ref in (rows_x, rows_g)
        )
        dg = dot_tn(xr, g).astype(BF)
        du = dot_tn(xr, u).astype(BF)
        dd = dot_tn(h, gr).astype(BF)
        for half in range(2):
            grad_g[half, e] = dg[half * LN : (half + 1) * LN]
            grad_u[half, e] = du[half * LN : (half + 1) * LN]
            grad_d[half, e] = dd[:, half * LN : (half + 1) * LN]
    mine = pl.ds(2 * core, 2)
    g_own = [
        pltpu.make_async_copy(grad_g.at[core], gg_ref.at[mine], sem_loc.at[0]),
        pltpu.make_async_copy(grad_u.at[core], gu_ref.at[mine], sem_loc.at[1]),
        pltpu.make_async_copy(grad_d.at[core], gd_ref.at[mine], sem_loc.at[2]),
    ]
    g_cp = [
        to_partner(5, grad_g.at[other], gg_ref.at[mine]),
        to_partner(6, grad_u.at[other], gu_ref.at[mine]),
        to_partner(7, grad_d.at[other], gd_ref.at[mine]),
    ]
    for cp in g_own + g_cp:
        cp.start()
    for i in range(NEXP):
        pltpu.make_async_copy(send_r.at[i], recv_r.at[i], sem_rr.at[i]).wait()

    sums = [None] * 4
    for c in range(COLS):
        value = recv_r[:, :, c * LN : (c + 1) * LN].reshape(NEXP * PR, LN).astype(F32)
        low = packet_row < 2 * c
        if c < 2:
            value = value * slot_gate[c]
        elif c == 2:
            value = value * jnp.where(low, slot_gate[c], 1.0)
        first = jnp.where(low, value, 0.0).astype(BF)
        second = jnp.where(low, 0.0, value).astype(BF)
        if c == 0:
            sums[0] = dot_tn(pick[c], second)
        elif c == COLS - 1:
            sums[3] = sums[3] + dot_tn(pick[c], first)
        else:
            got = dot_tn(pick[c], jnp.concatenate([first, second], axis=1))
            sums[c - 1] = sums[c - 1] + got[:, :LN]
            sums[c] = got[:, LN:]
    for q in range(4):
        fin[q] = sums[q]
    f_cp = [
        pltpu.make_async_remote_copy(
            fin.at[2 * i + other], recv_f.at[i], sem_fs.at[i], sem_fr.at[i],
            device_id=(partner, exp), device_id_type=MESH,
        )
        for i in range(2)
    ]
    for cp in f_cp:
        cp.start()
    for cp in tok_cp + w_cp + d_cp + r_cp:
        cp.wait_send()
    for s in range(GRP):
        for cp in p_cp[s] + h_cp[s] + [x_cp[s]]:
            cp.wait_send()
    for cp in g_own + g_cp + f_cp:
        cp.wait()
    out_ref[...] = (fin[core] + recv_f[0]).astype(BF)
    gtok_ref[...] = (fin[2 + core] + recv_f[1]).astype(BF)


def per_device(tokens, expert_ids, route_gates, w_gate, w_up, w_down, grad_out):
    vmem = pl.BlockSpec(memory_space=pltpu.VMEM)
    dma = pltpu.SemaphoreType.DMA
    return pl.pallas_call(
        kernel,
        out_shape=(
            jax.ShapeDtypeStruct((TOK, LN), BF),
            jax.ShapeDtypeStruct((TOK, LN), BF),
            jax.ShapeDtypeStruct((4, LN, FF), BF),
            jax.ShapeDtypeStruct((4, LN, FF), BF),
            jax.ShapeDtypeStruct((4, FF, LN), BF),
        ),
        in_specs=[vmem] * 7,
        out_specs=(vmem,) * 5,
        scratch_shapes=[
            pltpu.VMEM((4, TOK, LN), BF),
            pltpu.VMEM((2, 2, LN, FF), BF),
            pltpu.VMEM((2, 2, LN, FF), BF),
            pltpu.VMEM((2, 2, FF, LN), BF),
            pltpu.VMEM((128, TOK), F32),
            pltpu.VMEM((128, TOK), F32),
            pltpu.VMEM((COLS, NEXP * PR, TOK), BF),
            pltpu.VMEM((COLS, NEXP * PR, LN), F32),
            pltpu.VMEM((4, 2 * SH, 256), BF),
            pltpu.VMEM((4, 256, 2 * SH), BF),
            pltpu.VMEM((NEXP, PR, COLS * LN), BF),
            pltpu.VMEM((NEXP, PR, COLS * LN), BF),
            pltpu.VMEM((GRP, 2, SH, 2 * LN), BF),
            pltpu.VMEM((GRP, 2, SH, 2 * LN), BF),
            pltpu.VMEM((GRP, 4, SH, 3 * HALF), BF),
            pltpu.VMEM((GRP, 3, SH, 3 * HALF), BF),
            pltpu.VMEM((GRP, SH, 3 * HALF), BF),
            pltpu.VMEM((GRP, SH, 3 * HALF), BF),
            pltpu.VMEM((GRP, 4, SH, 3 * HALF), BF),
            pltpu.VMEM((NEXP, PR, COLS * LN), BF),
            pltpu.VMEM((NEXP, PR, COLS * LN), BF),
            pltpu.VMEM((2, 2, LN, FF), BF),
            pltpu.VMEM((2, 2, LN, FF), BF),
            pltpu.VMEM((2, 2, FF, LN), BF),
            pltpu.VMEM((4, TOK, LN), F32),
            pltpu.VMEM((2, TOK, LN), F32),
            dma((5,)),
            dma((8,)),
            dma((8,)),
            dma((NEXP,)),
            dma((NEXP,)),
            dma((GRP, 3)),
            dma((GRP, 3)),
            dma((GRP,)),
            dma((GRP,)),
            dma((GRP, 3)),
            dma((GRP, 3)),
            dma((NEXP,)),
            dma((NEXP,)),
            dma((2,)),
            dma((2,)),
        ],
        compiler_params=pltpu.CompilerParams(collective_id=0, has_side_effects=True),
        name="moe_block",
    )(tokens, expert_ids.T, route_gates.T, w_gate, w_up, w_down, grad_out)


def solution(mesh):
    return jax.shard_map(
        per_device,
        mesh=mesh,
        in_specs=(
            P("exp", "ctx"),
            P("exp", None),
            P("exp", None),
            P("exp", "ctx", None),
            P("exp", "ctx", None),
            P("exp", None, "ctx"),
            P("exp", "ctx"),
        ),
        out_specs=(
            P("exp", "ctx"),
            P("exp", "ctx"),
            P("exp", "ctx", None),
            P("exp", "ctx", None),
            P("exp", None, "ctx"),
        ),
        check_vma=False,
    )
```

```python
import jax
import jax.numpy as jnp
from jax import lax
from jax.experimental import pallas as pl
from jax.experimental.pallas import tpu as pltpu
from jax.sharding import PartitionSpec as P

CAP = 9
MESH = pl.DeviceIdType.MESH
BF = jnp.bfloat16
F32 = jnp.float32

TOK = 128
LN = 128
FF = 768
NEXP = 32
GRP = 4
COLS = 5
PR = 16
SLOTS = 18
SH = 72
HALF = FF // 2
OFFS = [
    (0, 0), (1, 0), (0, 1), (1, 1), (0, 15), (1, 15), (0, 2), (1, 2),
    (0, 8), (1, 8), (0, 7), (1, 7), (0, 9), (1, 9), (0, 6), (1, 6),
    (0, 10), (1, 10), (0, 5), (1, 5), (0, 11), (1, 11), (0, 12), (1, 12),
    (0, 4), (1, 4), (0, 3), (1, 3), (0, 13), (1, 13), (0, 14), (1, 14),
]
STEPS = "DPDSPFDSDPGFPSOGFSOGFOGO"


def dot(a, b):
    return lax.dot_general(a, b, (((1,), (0,)), ((), ())), preferred_element_type=F32)


def dot_tn(a, b):
    return lax.dot_general(a, b, (((0,), (0,)), ((), ())), preferred_element_type=F32)


def dot_nt(a, b):
    return lax.dot_general(a, b, (((1,), (1,)), ((), ())), preferred_element_type=F32)


def iota(shape, dim):
    return lax.broadcasted_iota(jnp.int32, shape, dim)


def packet_target(q, index):
    col = (index >= 128).astype(jnp.int32)
    rest = index - 128 * col
    source = rest // PR
    place = PR * (q + col) + rest % PR - SLOTS * q
    second = (place >= CAP).astype(jnp.int32)
    target = second * 72 + source * CAP + place - CAP * second
    return jnp.where((place >= 0) & (place < SLOTS), target, -1)


def kernel(
    tok_ref, ids_ref, gates_ref, wg_ref, wu_ref, wd_ref, gout_ref,
    out_ref, gtok_ref, gg_ref, gu_ref, gd_ref,
    xg, wgb, wub, wdb, pos_t, gate_t, pick, slot_gate, perm, perm_t,
    send_d, recv_d, rows_x, rows_g, part, recv_q, recv_p, sum_s, sum_r, hid,
    send_r, recv_r, grad_g, grad_u, grad_d, fin, recv_f,
    sem_loc, sem_cs, sem_cr, sem_ds, sem_dr, sem_qs, sem_qr, sem_ps, sem_pr,
    sem_xs, sem_xr, sem_hs, sem_hr, sem_gs, sem_gr,
    sem_rs, sem_rr, sem_fs, sem_fr,
):
    ctx = lax.axis_index("ctx")
    exp = lax.axis_index("exp")
    core = ctx % 2
    other = 1 - core
    y_at = (ctx // 2) % 4
    x_hi = ctx // 8
    x_lo = exp // 16
    z_at = exp % 16
    partner = ctx - core + other
    across = ctx - 8 * x_hi + 8 * (1 - x_hi)

    def exp_at(x, z):
        return ((x_lo + x) % 2) * 16 + (z_at + z) % 16

    def y_dev(d):
        return 8 * x_hi + 2 * ((y_at + d) % 4) + core

    barrier = pltpu.get_barrier_semaphore()
    pl.semaphore_signal(barrier, 1, device_id=(partner, exp), device_id_type=MESH)
    for x, z in OFFS[::-1]:
        if (x, z) != (0, 0):
            pl.semaphore_signal(barrier, 1, device_id=(ctx, exp_at(x, z)), device_id_type=MESH)
    for d in (1, 3):
        pl.semaphore_signal(barrier, 1, device_id=(y_dev(d), exp), device_id_type=MESH)
    pl.semaphore_signal(barrier, 1, device_id=(across, exp), device_id_type=MESH)

    local = [
        pltpu.make_async_copy(tok_ref, xg.at[core], sem_loc.at[0]),
        pltpu.make_async_copy(gout_ref, xg.at[2 + core], sem_loc.at[1]),
        pltpu.make_async_copy(wg_ref.at[pl.ds(2 * core, 2)], wgb.at[core], sem_loc.at[2]),
        pltpu.make_async_copy(wu_ref.at[pl.ds(2 * core, 2)], wub.at[core], sem_loc.at[3]),
        pltpu.make_async_copy(wd_ref.at[pl.ds(2 * core, 2)], wdb.at[core], sem_loc.at[4]),
    ]
    for cp in local:
        cp.start()

    row = iota((128, TOK), 0)
    expert = jnp.where(row < 64, 4 * (row % 32) + 2 * core + row // 32, -1)
    hit = jnp.zeros((128, TOK), F32)
    gate = jnp.zeros((128, TOK), F32)
    for k in range(8):
        same = ids_ref[k : k + 1, :] == expert
        hit = hit + same.astype(F32)
        gate = gate + jnp.where(same, gates_ref[k : k + 1, :], 0.0)
    earlier = (iota((TOK, TOK), 0) < iota((TOK, TOK), 1)).astype(F32).astype(BF)
    pos_t[...] = jnp.where(hit > 0.5, dot(hit.astype(BF), earlier), -1.0)
    gate_t[...] = gate

    def build(d, carry):
        p0 = pos_t[pl.ds(d, 1), :]
        p1 = pos_t[pl.ds(d + NEXP, 1), :]
        g0 = gate_t[pl.ds(d, 1), :]
        g1 = gate_t[pl.ds(d + NEXP, 1), :]
        at = pl.ds(pl.multiple_of(d * PR, PR), PR)
        for c in range(COLS):
            row = iota((PR, TOK), 0) + PR * c
            quarter = jnp.where(row >= SLOTS * c, c, c - 1)
            slot = row - SLOTS * quarter
            second = slot >= CAP
            wanted = jnp.where(second, slot - CAP, slot).astype(F32)
            if c == COLS - 1:
                wanted = jnp.where(row < 4 * SLOTS, wanted, -2.0)
            chosen = jnp.where(second, p1, p0) == wanted
            pick[c, at, :] = chosen.astype(F32).astype(BF)
            weight = jnp.sum(
                jnp.where(chosen, jnp.where(second, g1, g0), 0.0), axis=1, keepdims=True
            )
            slot_gate[c, at, :] = jnp.broadcast_to(weight, (PR, 128))
        return carry

    lax.fori_loop(0, NEXP, build, 0)
    for q in range(4):
        perm[q] = (
            (packet_target(q, iota((2 * SH, 256), 1)) == iota((2 * SH, 256), 0))
            .astype(F32).astype(BF)
        )
        perm_t[q] = (
            (packet_target(q, iota((256, 2 * SH), 0)) == iota((256, 2 * SH), 1))
            .astype(F32).astype(BF)
        )

    for cp in local:
        cp.wait()
    pl.semaphore_wait(barrier, 1 + (NEXP - 1) + 2 + 1)

    def to_partner(i, src, dst):
        return pltpu.make_async_remote_copy(
            src, dst, sem_cs.at[i], sem_cr.at[i], device_id=(partner, exp), device_id_type=MESH
        )

    tok_cp = [to_partner(0, tok_ref, xg.at[core]), to_partner(1, gout_ref, xg.at[2 + core])]
    w_cp = [
        to_partner(2, wg_ref.at[pl.ds(2 * other, 2)], wgb.at[core]),
        to_partner(3, wu_ref.at[pl.ds(2 * other, 2)], wub.at[core]),
        to_partner(4, wd_ref.at[pl.ds(2 * other, 2)], wdb.at[core]),
    ]
    for cp in tok_cp + w_cp:
        cp.start()
    for cp in tok_cp:
        cp.wait_recv()

    packet_row = iota((NEXP * PR, LN), 0) % PR
    for c in range(COLS):
        low = packet_row < 2 * c
        if c == 0:
            rows = dot(pick[c], xg[0])
        elif c == COLS - 1:
            rows = dot(pick[c], xg[3])
        else:
            both = dot(pick[c], jnp.concatenate([xg[c - 1], xg[c]], axis=1))
            rows = jnp.where(low, both[:, :LN], both[:, LN:])
        if c == 2:
            rows = rows * jnp.where(low, 1.0, slot_gate[c])
        elif c > 2:
            rows = rows * slot_gate[c]
        send_d[:, :, c * LN : (c + 1) * LN] = rows.astype(BF).reshape(NEXP, PR, LN)

    d_cp = []
    for i, (x, z) in enumerate(OFFS):
        to = exp_at(x, 16 - z)
        if (x, z) == (0, 0):
            cp = pltpu.make_async_copy(send_d.at[exp], recv_d.at[i], sem_dr.at[i])
        else:
            cp = pltpu.make_async_remote_copy(
                send_d.at[to], recv_d.at[i], sem_ds.at[i], sem_dr.at[i],
                device_id=(ctx, to), device_id_type=MESH,
            )
            d_cp.append(cp)
        cp.start()
    for cp in w_cp:
        cp.wait_recv()

    def w_cols(ref, e):
        return jnp.concatenate([ref[0, e], ref[1, e]], axis=0)

    def w_rows(e):
        return jnp.concatenate([wdb[0, e], wdb[1, e]], axis=1)

    up, down, far = (y_at + 1) % 4, (y_at + 3) % 4, (y_at + 2) % 4

    def y_send(s, n, src, dst, sem_s, sem_r):
        cp = pltpu.make_async_remote_copy(
            src, dst, sem_s.at[s, n], sem_r.at[s, n],
            device_id=(y_dev(1 if n == 0 else 3), exp), device_id_type=MESH,
        )
        cp.start()
        return cp

    def cut(s, n):
        at = 5 * LN if s % 2 == 0 else 4 * LN
        return slice(0, at) if n == 0 else slice(at, 3 * HALF)

    q_cp, p_cp, x_cp, h_cp, f_cp, r_cp = {}, {}, {}, {}, {}, []

    def step_d(s):
        for i in range(8 * s, 8 * s + 8):
            pltpu.make_async_copy(send_d.at[i], recv_d.at[i], sem_dr.at[i]).wait()
        cols = [
            recv_d[8 * s : 8 * s + 8, :, c * LN : (c + 1) * LN].reshape(128, LN)
            for c in range(COLS)
        ]
        for q in range(4):
            got = dot(perm[q], jnp.concatenate(cols[q : q + 2], axis=0))
            into = rows_x if q < 2 else rows_g
            for e in range(2):
                into[s, e, :, (q % 2) * LN : (q % 2 + 1) * LN] = got[
                    e * SH : (e + 1) * SH
                ].astype(BF)
        for e in range(2):
            made = (
                dot(rows_x[s, e], w_cols(wgb, e)),
                dot(rows_x[s, e], w_cols(wub, e)),
                dot_nt(rows_g[s, e], w_rows(e)),
            )
            for n, value in enumerate(made):
                value = value.astype(BF)
                for side in range(2):
                    part[s, 2 * e + side, :, n * HALF : (n + 1) * HALF] = value[
                        :, side * HALF : (side + 1) * HALF
                    ]
        q_cp[s] = [
            y_send(
                s, n, part.at[s, far, :, cut(s, n)], recv_q.at[s, :, cut(s, n)], sem_qs, sem_qr
            )
            for n in range(2)
        ]

    def step_p(s):
        p_cp[s] = []
        for n, to in enumerate((up, down)):
            q_cp[s][n].wait_recv()
            at = cut(s, n)
            part[s, to, :, at] = (
                part[s, to, :, at].astype(F32) + recv_q[s, :, at].astype(F32)
            ).astype(BF)
            p_cp[s].append(y_send(s, n, part.at[s, to], recv_p.at[s, n], sem_ps, sem_pr))

    def step_s(s):
        for cp in p_cp[s]:
            cp.wait_recv()
        total = part[s, y_at].astype(F32)
        for d in range(2):
            total = total + recv_p[s, d].astype(F32)
        sum_s[s] = total.astype(BF)
        x_cp[s] = pltpu.make_async_remote_copy(
            sum_s.at[s], sum_r.at[s], sem_xs.at[s], sem_xr.at[s],
            device_id=(across, exp), device_id_type=MESH,
        )
        x_cp[s].start()

    def step_f(s):
        x_cp[s].wait_recv()
        total = sum_s[s].astype(F32) + sum_r[s].astype(F32)
        gate_sum, up_sum, back_sum = (total[:, n * HALF : (n + 1) * HALF] for n in range(3))
        sig = jax.nn.sigmoid(gate_sum)
        silu = gate_sum * sig
        hid[s, y_at, :, 0:HALF] = (silu * up_sum).astype(BF)
        hid[s, y_at, :, HALF : 2 * HALF] = (
            back_sum * up_sum * sig * (1.0 + gate_sum * (1.0 - sig))
        ).astype(BF)
        hid[s, y_at, :, 2 * HALF : 3 * HALF] = (back_sum * silu).astype(BF)
        h_cp[s] = [
            y_send(s, n, hid.at[s, y_at], hid.at[s, y_at], sem_hs, sem_hr) for n in range(2)
        ]

    def step_g(s):
        f_cp[s] = []
        for n, of in enumerate((down, up)):
            h_cp[s][n].wait_recv()
            piece = hid.at[s, of, :, cut(s, n)]
            f_cp[s].append(y_send(s, n, piece, piece, sem_gs, sem_gr))

    def hid_rows(s, e, n):
        at = slice(n * HALF, (n + 1) * HALF)
        return jnp.concatenate([hid[s, 2 * e, :, at], hid[s, 2 * e + 1, :, at]], axis=1)

    def step_o(s):
        for cp in f_cp[s]:
            cp.wait_recv()
        made = []
        for e in range(2):
            h, g, u = (hid_rows(s, e, n) for n in range(3))
            made.append(
                (
                    dot(h, w_rows(e)).astype(BF),
                    (dot_nt(g, w_cols(wgb, e)) + dot_nt(u, w_cols(wub, e))).astype(BF),
                )
            )
        back = [
            jnp.concatenate(
                [made[e][q // 2][:, (q % 2) * LN : (q % 2 + 1) * LN].astype(F32) for e in range(2)],
                axis=0,
            ).astype(BF)
            for q in range(4)
        ]
        for c in range(COLS):
            value = None
            for q in (c - 1, c):
                if 0 <= q < 4:
                    term = dot(perm_t[q, (c - q) * 128 : (c - q + 1) * 128, :], back[q])
                    value = term if value is None else value + term
            send_r[8 * s : 8 * s + 8, :, c * LN : (c + 1) * LN] = value.astype(BF).reshape(
                8, PR, LN
            )
        for i in range(8 * s, 8 * s + 8):
            x, z = OFFS[i]
            to = exp_at(x, z)
            if (x, z) == (0, 0):
                cp = pltpu.make_async_copy(send_r.at[i], recv_r.at[exp], sem_rr.at[i])
            else:
                cp = pltpu.make_async_remote_copy(
                    send_r.at[i], recv_r.at[exp], sem_rs.at[i], sem_rr.at[i],
                    device_id=(ctx, to), device_id_type=MESH,
                )
                r_cp.append(cp)
            cp.start()

    do = {"D": step_d, "P": step_p, "S": step_s, "F": step_f, "G": step_g, "O": step_o}
    for n, step in enumerate(STEPS):
        do[step](STEPS[:n].count(step))

    for e in range(2):
        h, g, u = (
            jnp.concatenate([hid_rows(s, e, n).astype(F32) for s in range(GRP)], axis=0).astype(BF)
            for n in range(3)
        )
        xr, gr = (
            jnp.concatenate([ref[s, e].astype(F32) for s in range(GRP)], axis=0).astype(BF)
            for ref in (rows_x, rows_g)
        )
        dg = dot_tn(xr, g).astype(BF)
        du = dot_tn(xr, u).astype(BF)
        dd = dot_tn(h, gr).astype(BF)
        for half in range(2):
            grad_g[half, e] = dg[half * LN : (half + 1) * LN]
            grad_u[half, e] = du[half * LN : (half + 1) * LN]
            grad_d[half, e] = dd[:, half * LN : (half + 1) * LN]
    mine = pl.ds(2 * core, 2)
    g_own = [
        pltpu.make_async_copy(grad_g.at[core], gg_ref.at[mine], sem_loc.at[0]),
        pltpu.make_async_copy(grad_u.at[core], gu_ref.at[mine], sem_loc.at[1]),
        pltpu.make_async_copy(grad_d.at[core], gd_ref.at[mine], sem_loc.at[2]),
    ]
    g_cp = [
        to_partner(5, grad_g.at[other], gg_ref.at[mine]),
        to_partner(6, grad_u.at[other], gu_ref.at[mine]),
        to_partner(7, grad_d.at[other], gd_ref.at[mine]),
    ]
    for cp in g_own + g_cp:
        cp.start()
    for i in range(NEXP):
        pltpu.make_async_copy(send_r.at[i], recv_r.at[i], sem_rr.at[i]).wait()

    sums = [None] * 4
    for c in range(COLS):
        value = recv_r[:, :, c * LN : (c + 1) * LN].reshape(NEXP * PR, LN).astype(F32)
        low = packet_row < 2 * c
        if c < 2:
            value = value * slot_gate[c]
        elif c == 2:
            value = value * jnp.where(low, slot_gate[c], 1.0)
        first = jnp.where(low, value, 0.0).astype(BF)
        second = jnp.where(low, 0.0, value).astype(BF)
        if c == 0:
            sums[0] = dot_tn(pick[c], second)
        elif c == COLS - 1:
            sums[3] = sums[3] + dot_tn(pick[c], first)
        else:
            got = dot_tn(pick[c], jnp.concatenate([first, second], axis=1))
            sums[c - 1] = sums[c - 1] + got[:, :LN]
            sums[c] = got[:, LN:]
    for q in range(4):
        fin[q] = sums[q]
    e_cp = [
        pltpu.make_async_remote_copy(
            fin.at[2 * i + other], recv_f.at[i], sem_fs.at[i], sem_fr.at[i],
            device_id=(partner, exp), device_id_type=MESH,
        )
        for i in range(2)
    ]
    for cp in e_cp:
        cp.start()
    for cp in tok_cp + w_cp + d_cp + r_cp:
        cp.wait_send()
    for s in range(GRP):
        for cp in q_cp[s] + p_cp[s] + h_cp[s] + f_cp[s] + [x_cp[s]]:
            cp.wait_send()
    for cp in g_own + g_cp + e_cp:
        cp.wait()
    out_ref[...] = (fin[core] + recv_f[0]).astype(BF)
    gtok_ref[...] = (fin[2 + core] + recv_f[1]).astype(BF)


def per_device(tokens, expert_ids, route_gates, w_gate, w_up, w_down, grad_out):
    vmem = pl.BlockSpec(memory_space=pltpu.VMEM)
    dma = pltpu.SemaphoreType.DMA
    return pl.pallas_call(
        kernel,
        out_shape=(
            jax.ShapeDtypeStruct((TOK, LN), BF),
            jax.ShapeDtypeStruct((TOK, LN), BF),
            jax.ShapeDtypeStruct((4, LN, FF), BF),
            jax.ShapeDtypeStruct((4, LN, FF), BF),
            jax.ShapeDtypeStruct((4, FF, LN), BF),
        ),
        in_specs=[vmem] * 7,
        out_specs=(vmem,) * 2 + (pl.BlockSpec(memory_space=pl.ANY),) * 3,
        scratch_shapes=[
            pltpu.VMEM((4, TOK, LN), BF),
            pltpu.VMEM((2, 2, LN, FF), BF),
            pltpu.VMEM((2, 2, LN, FF), BF),
            pltpu.VMEM((2, 2, FF, LN), BF),
            pltpu.VMEM((128, TOK), F32),
            pltpu.VMEM((128, TOK), F32),
            pltpu.VMEM((COLS, NEXP * PR, TOK), BF),
            pltpu.VMEM((COLS, NEXP * PR, LN), F32),
            pltpu.VMEM((4, 2 * SH, 256), BF),
            pltpu.VMEM((4, 256, 2 * SH), BF),
            pltpu.VMEM((NEXP, PR, COLS * LN), BF),
            pltpu.VMEM((NEXP, PR, COLS * LN), BF),
            pltpu.VMEM((GRP, 2, SH, 2 * LN), BF),
            pltpu.VMEM((GRP, 2, SH, 2 * LN), BF),
            pltpu.VMEM((GRP, 4, SH, 3 * HALF), BF),
            pltpu.VMEM((GRP, SH, 3 * HALF), BF),
            pltpu.VMEM((GRP, 2, SH, 3 * HALF), BF),
            pltpu.VMEM((GRP, SH, 3 * HALF), BF),
            pltpu.VMEM((GRP, SH, 3 * HALF), BF),
            pltpu.VMEM((GRP, 4, SH, 3 * HALF), BF),
            pltpu.VMEM((NEXP, PR, COLS * LN), BF),
            pltpu.VMEM((NEXP, PR, COLS * LN), BF),
            pltpu.VMEM((2, 2, LN, FF), BF),
            pltpu.VMEM((2, 2, LN, FF), BF),
            pltpu.VMEM((2, 2, FF, LN), BF),
            pltpu.VMEM((4, TOK, LN), F32),
            pltpu.VMEM((2, TOK, LN), F32),
            dma((5,)),
            dma((8,)),
            dma((8,)),
            dma((NEXP,)),
            dma((NEXP,)),
            dma((GRP, 2)),
            dma((GRP, 2)),
            dma((GRP, 2)),
            dma((GRP, 2)),
            dma((GRP,)),
            dma((GRP,)),
            dma((GRP, 2)),
            dma((GRP, 2)),
            dma((GRP, 2)),
            dma((GRP, 2)),
            dma((NEXP,)),
            dma((NEXP,)),
            dma((2,)),
            dma((2,)),
        ],
        compiler_params=pltpu.CompilerParams(
            collective_id=0, has_side_effects=True, vmem_limit_bytes=36 << 20
        ),
        name="moe_block",
    )(tokens, expert_ids.T, route_gates.T, w_gate, w_up, w_down, grad_out)


def solution(mesh):
    return jax.shard_map(
        per_device,
        mesh=mesh,
        in_specs=(
            P("exp", "ctx"),
            P("exp", None),
            P("exp", None),
            P("exp", "ctx", None),
            P("exp", "ctx", None),
            P("exp", None, "ctx"),
            P("exp", "ctx"),
        ),
        out_specs=(
            P("exp", "ctx"),
            P("exp", "ctx"),
            P("exp", "ctx", None),
            P("exp", "ctx", None),
            P("exp", None, "ctx"),
        ),
        check_vma=False,
    )
```
